256 devices in a mesh: row: 16 (over z, core), col: 16 (over y, x).
Axes of the slice: x: 4, y: 4, z: 8, core: 2. Of those that a mesh axis runs over, the one named last changes fastest.
Arguments:
- clean_in: bfloat16 [512, 8192], P('row', 'col'), may hold values from -6 to 6
- corrupt_in: bfloat16 [512, 8192], P('row', 'col'), may hold values from -6 to 6
- patch_mask: int32 [512], replicated, may hold values 0 or 1
- gate_weight: bfloat16 [8192, 28672], P('col', 'row'), may hold values from -0.0625 to 0.0625
- up_weight: bfloat16 [8192, 28672], P('col', 'row'), may hold values from -0.0625 to 0.0625
- down_weight: bfloat16 [28672, 8192], P('row', 'col'), may hold values from -0.03125 to 0.03125
Outputs:
- clean_out: float32 [512, 8192], P('row', 'col')
- patched_out: float32 [512, 8192], P('row', 'col')
The draws below stay inside these ranges and needn't reach their ends.
All inputs are finite; a program needn't handle non-finite values.
Results may differ from the reference program's by a relative error of at most 0.0029.
Values may be sent and summed in bfloat16 or wider, within the bound.
A program may use at most 128 MiB of HBM per device.

```python
import jax
import jax.numpy as jnp

D = 8192
FF = 28672
TOK = 512


def set_ends(entries, key, smallest, largest):
    place = [jax.random.randint(jax.random.fold_in(key, axis), (), 0, length) for axis, length in enumerate(entries.shape)]
    widest = entries.shape.index(max(entries.shape))
    beside = place[:widest] + [(place[widest] + 1) % entries.shape[widest]] + place[widest + 1:]
    return entries.at[tuple(place)].set(smallest).at[tuple(beside)].set(largest)


def level_of(rng, extent, shards, low, high):
    gain, own = 1.0, jax.random.fold_in(rng, 6)
    for dim, parts in shards:
        heights = jnp.exp(jax.random.uniform(jax.random.fold_in(own, dim), (parts,), jnp.float32, low / len(shards), high / len(shards)))
        gain = gain * jnp.repeat(heights, extent[dim] // parts).reshape([-1 if axis == dim else 1 for axis in range(len(extent))])
    return gain


def bell_draw(own_key, dims, width, most, shards=(), dtype=jnp.bfloat16):
    array = width * jax.random.normal(own_key, dims, jnp.float32)
    if shards:
        array = array * level_of(own_key, dims, shards, -0.22, 0.18)
    return jnp.clip(array, -most, most).astype(dtype)


def setup_inputs(seed: int = 0) -> dict:
    streams_of = jax.random.split(jax.random.key(seed), 7)
    clean_in = bell_draw(streams_of[0], (TOK, D), 1.0, 6.0, ((0, 16), (1, 16)))
    corrupt_in = bell_draw(streams_of[1], (TOK, D), 1.0, 6.0, ((0, 16), (1, 16)))
    patch_mask = set_ends((jax.random.randint(streams_of[2], (TOK,), 0, 2) < 1).astype(jnp.int32), jax.random.fold_in(streams_of[2], 1), 0, 1)
    gate_weight = bell_draw(streams_of[3], (D, FF), D ** -0.5, 0.0625, ((0, 16), (1, 16)))
    up_weight = bell_draw(streams_of[4], (D, FF), D ** -0.5, 0.0625, ((0, 16), (1, 16)))
    down_weight = bell_draw(streams_of[5], (FF, D), FF ** -0.5, 0.03125, ((0, 16), (1, 16)))
    return dict(clean_in=clean_in, corrupt_in=corrupt_in, patch_mask=patch_mask, gate_weight=gate_weight, up_weight=up_weight, down_weight=down_weight)


def hidden_of(inputs, gate_weight, up_weight):
    gate_part = jnp.dot(inputs, gate_weight, preferred_element_type=jnp.float32)
    up_part = jnp.dot(inputs, up_weight, preferred_element_type=jnp.float32)
    return (jax.nn.silu(gate_part) * up_part).astype(jnp.bfloat16)


def reference(clean_in, corrupt_in, patch_mask, gate_weight, up_weight, down_weight):
    hidden_clean = hidden_of(clean_in, gate_weight, up_weight)
    hidden_corrupt = hidden_of(corrupt_in, gate_weight, up_weight)
    hidden_patched = jnp.where(patch_mask[:, None] == 1, hidden_clean, hidden_corrupt)
    clean_out = jnp.dot(hidden_clean, down_weight, preferred_element_type=jnp.float32)
    patched_out = jnp.dot(hidden_patched, down_weight, preferred_element_type=jnp.float32)
    return (clean_out, patched_out)
```

```python
import jax
import jax.numpy as jnp
from jax import lax
from jax.experimental import pallas as pl
from jax.experimental.pallas import tpu as pltpu
from jax.sharding import PartitionSpec as P

MESH = pl.DeviceIdType.MESH
ZN = 8
XN = 4


def remote(src, dst, send, recv, axis, index):
    return pltpu.make_async_remote_copy(
        src_ref=src, dst_ref=dst, send_sem=send, recv_sem=recv,
        device_id={axis: index}, device_id_type=MESH,
    )


def greet(axis, peers):
    barrier = pltpu.get_barrier_semaphore()
    for peer in peers:
        pl.semaphore_signal(barrier, inc=1, device_id={axis: peer}, device_id_type=MESH)
    pl.semaphore_wait(barrier, len(peers))


def gather_row_kernel(clean_ref, corrupt_ref, out_ref, local_sem, send_sem, recv_sem, pair_send, pair_recv):
    me = lax.axis_index("row")
    z, core = me // 2, me % 2
    right = ((z + 1) % ZN) * 2 + core
    left = ((z + ZN - 1) % ZN) * 2 + core
    pair = z * 2 + (1 - core)
    first = pltpu.make_async_copy(clean_ref, out_ref.at[me, 0], local_sem.at[0])
    second = pltpu.make_async_copy(corrupt_ref, out_ref.at[me, 1], local_sem.at[1])
    first.start()
    second.start()
    greet("row", (left, right, pair))
    first.wait()
    second.wait()

    def chain(way, step, block):
        view = out_ref.at[block] if step < 3 else out_ref.at[block, way]
        return remote(view, view, send_sem.at[way, step], recv_sem.at[way, step], "row", (right, left)[way])

    def hand(slot, view):
        return remote(view, view, pair_send.at[slot], pair_recv.at[slot], "row", pair)

    started = []

    def go(copy):
        copy.start()
        started.append(copy)

    go(chain(0, 0, me))
    go(chain(1, 0, me))
    go(hand(0, out_ref.at[me]))
    for step in range(4):
        for way in range(2):
            away = (ZN - step - 1) if way == 0 else (step + 1)
            block = ((z + away) % ZN) * 2 + core
            chain(way, step, block).wait_recv()
            if step < 3:
                go(chain(way, step + 1, block))
            view = out_ref.at[block] if step < 3 else out_ref.at[block, way]
            go(hand(1 + step * 2 + way, view))
    hand(0, out_ref.at[pair]).wait_recv()
    for step in range(4):
        for way in range(2):
            away = (ZN - step - 1) if way == 0 else (step + 1)
            block = ((z + away) % ZN) * 2 + (1 - core)
            view = out_ref.at[block] if step < 3 else out_ref.at[block, way]
            hand(1 + step * 2 + way, view).wait_recv()
    for copy in started:
        copy.wait_send()


def gather_row(clean, corrupt):
    rows, width = clean.shape
    return pl.pallas_call(
        gather_row_kernel,
        out_shape=jax.ShapeDtypeStruct((2 * ZN, 2, rows, width), clean.dtype),
        in_specs=[pl.BlockSpec(memory_space=pl.ANY)] * 2,
        out_specs=pl.BlockSpec(memory_space=pltpu.VMEM),
        scratch_shapes=[
            pltpu.SemaphoreType.DMA((2,)),
            pltpu.SemaphoreType.DMA((2, 4)),
            pltpu.SemaphoreType.DMA((2, 4)),
            pltpu.SemaphoreType.DMA((9,)),
            pltpu.SemaphoreType.DMA((9,)),
        ],
        compiler_params=pltpu.CompilerParams(collective_id=0, has_side_effects=True),
        name="gather_row",
    )(clean, corrupt)


def gather_col_kernel(own_ref, out_ref, local_sem, send_sem, recv_sem):
    me = lax.axis_index("col")
    y, x = me // XN, me % XN
    half = own_ref.shape[1] // 2

    def at(dy, dx):
        return ((y + dy) % XN) * XN + (x + dx) % XN

    local = pltpu.make_async_copy(own_ref, out_ref.at[me], local_sem.at[0])
    local.start()
    greet("col", (at(0, 1), at(0, XN - 1), at(1, 0), at(XN - 1, 0)))
    local.wait()

    started = []

    def neighbour(run, stage, way):
        step = 1 if way == 0 else XN - 1
        along_x = (run + stage) % 2 == 0
        return at(0, step) if along_x else at(step, 0)

    def block_of(run, lane, hop):
        return at(hop, lane) if run == 0 else at(lane, hop)

    def copy_of(run, group, way, far, block):
        stage = 0 if group == 0 else 1
        view = out_ref.at[block, run]
        if far:
            view = out_ref.at[block, run, pl.ds(way * half, half)]
        sems = (run, group, way * 2 + far)
        return remote(view, view, send_sem.at[sems], recv_sem.at[sems], "col", neighbour(run, stage, way))

    def go(*key):
        copy = copy_of(*key)
        copy.start()
        started.append(copy)

    def second(run, lane):
        block = block_of(run, lane, 0)
        for way in range(2):
            go(run, 1 + lane, way, 0, block)

    for run in range(2):
        for way in range(2):
            go(run, 0, way, 0, me)
    for run in range(2):
        second(run, 0)
    for way in range(2):
        lane = XN - 1 if way == 0 else 1
        for run in range(2):
            block = block_of(run, lane, 0)
            copy_of(run, 0, way, 0, block).wait_recv()
            go(run, 0, way, 1, block)
            second(run, lane)

    def relay(run, lane):
        for way in range(2):
            hop = XN - 1 if way == 0 else 1
            block = block_of(run, lane, hop)
            copy_of(run, 1 + lane, way, 0, block).wait_recv()
            go(run, 1 + lane, way, 1, block)

    for run in range(2):
        relay(run, 0)
    for run in range(2):
        block = block_of(run, 2, 0)
        for way in range(2):
            copy_of(run, 0, way, 1, block).wait_recv()
        second(run, 2)
    for lane in (3, 1, 2):
        for run in range(2):
            relay(run, lane)
    for lane in range(XN):
        for run in range(2):
            for way in range(2):
                copy_of(run, 1 + lane, way, 1, block_of(run, lane, 2)).wait_recv()
    for copy in started:
        copy.wait_send()


def gather_col(paired):
    return pl.pallas_call(
        gather_col_kernel,
        out_shape=jax.ShapeDtypeStruct((XN * XN,) + paired.shape, paired.dtype),
        in_specs=[pl.BlockSpec(memory_space=pl.ANY)],
        out_specs=pl.BlockSpec(memory_space=pltpu.VMEM),
        scratch_shapes=[
            pltpu.SemaphoreType.DMA((1,)),
            pltpu.SemaphoreType.DMA((2, 1 + XN, 4)),
            pltpu.SemaphoreType.DMA((2, 1 + XN, 4)),
        ],
        compiler_params=pltpu.CompilerParams(collective_id=1, has_side_effects=True),
        name="gather_col",
    )(paired)


def scatter_row_kernel(part_ref, clean_ref, patched_ref, pair_buf, out_buf, in_buf, pair_send, pair_recv, send_sem, recv_sem):
    me = lax.axis_index("row")
    z, core = me // 2, me % 2
    pair = z * 2 + (1 - core)
    peers = [((z + d) % ZN) * 2 + core for d in range(1, ZN)]
    greet("row", [pair] + peers)
    order = (4, 3, 5, 2, 6, 1, 7, 0)

    def hand(d):
        target = ((z + d) % ZN) * 2 + (1 - core)
        return remote(part_ref.at[target], pair_buf.at[d], pair_send.at[d], pair_recv.at[d], "row", pair)

    def cast(d):
        return remote(out_buf.at[d], in_buf.at[d], send_sem.at[d], recv_sem.at[d], "row", ((z + d) % ZN) * 2 + core)

    for d in order:
        hand(d).start()
    for d in order[:-1]:
        hand(d).wait_recv()
        mine = ((z + d) % ZN) * 2 + core
        out_buf[d] = (part_ref[mine] + pair_buf[d]).astype(out_buf.dtype)
        cast(d).start()
    hand(0).wait_recv()
    total = part_ref[me] + pair_buf[0]
    clean_ref[...] = total[0]
    patched_ref[...] = total[1]
    for d in (1, 7, 2, 6, 3, 5, 4):
        cast(d).wait_recv()
        clean_ref[...] += in_buf[d, 0].astype(jnp.float32)
        patched_ref[...] += in_buf[d, 1].astype(jnp.float32)
    for d in range(ZN):
        hand(d).wait_send()
    for d in range(1, ZN):
        cast(d).wait_send()


def scatter_row(part):
    block = part.shape[1:]
    out = jax.ShapeDtypeStruct(block[1:], jnp.float32)
    return pl.pallas_call(
        scatter_row_kernel,
        out_shape=(out, out),
        in_specs=[pl.BlockSpec(memory_space=pltpu.VMEM)],
        out_specs=(pl.BlockSpec(memory_space=pltpu.VMEM), pl.BlockSpec(memory_space=pltpu.VMEM)),
        scratch_shapes=[
            pltpu.VMEM((ZN,) + block, jnp.float32),
            pltpu.VMEM((ZN,) + block, jnp.bfloat16),
            pltpu.VMEM((ZN,) + block, jnp.bfloat16),
            pltpu.SemaphoreType.DMA((ZN,)),
            pltpu.SemaphoreType.DMA((ZN,)),
            pltpu.SemaphoreType.DMA((ZN,)),
            pltpu.SemaphoreType.DMA((ZN,)),
        ],
        compiler_params=pltpu.CompilerParams(collective_id=2, has_side_effects=True),
        name="scatter_row",
    )(part)


def on_device(clean_in, corrupt_in, patch_mask, gate_weight, up_weight, down_weight):
    rows, width = clean_in.shape
    piece = gather_row(clean_in, corrupt_in).reshape(-1, width)
    gate_part = jnp.dot(piece, gate_weight, preferred_element_type=jnp.float32)
    gate = lax.psum_scatter(gate_part, "col", scatter_dimension=0, tiled=True)
    up_part = jnp.dot(piece, up_weight, preferred_element_type=jnp.float32)
    up = lax.psum_scatter(up_part, "col", scatter_dimension=0, tiled=True)
    row_mask = lax.dynamic_slice_in_dim(patch_mask, lax.axis_index("col") * rows, rows, 0)
    hidden = (jax.nn.silu(gate) * up).astype(jnp.bfloat16).reshape(2, rows, -1)
    patched = jnp.where(row_mask[:, None] == 1, hidden[0], hidden[1])
    gathered = gather_col(jnp.stack((hidden[0], patched)))
    part = jnp.dot(gathered.reshape(-1, gathered.shape[-1]), down_weight, preferred_element_type=jnp.float32)
    return scatter_row(part.reshape(2 * ZN, 2, rows, -1))


def solution(mesh):
    placed = (
        P("row", "col"),
        P("row", "col"),
        P(),
        P("col", "row"),
        P("col", "row"),
        P("row", "col"),
    )
    return jax.shard_map(
        on_device,
        mesh=mesh,
        in_specs=placed,
        out_specs=(P("row", "col"), P("row", "col")),
        check_vma=False,
    )
```

```python
import jax
import jax.numpy as jnp
from jax import lax
from jax.experimental import pallas as pl
from jax.experimental.pallas import tpu as pltpu
from jax.sharding import PartitionSpec as P

MESH = pl.DeviceIdType.MESH
ZN = 8
XN = 4


def remote(src, dst, send, recv, axis, index):
    return pltpu.make_async_remote_copy(
        src_ref=src, dst_ref=dst, send_sem=send, recv_sem=recv,
        device_id={axis: index}, device_id_type=MESH,
    )


def greet(axis, peers):
    barrier = pltpu.get_barrier_semaphore()
    for peer in peers:
        pl.semaphore_signal(barrier, inc=1, device_id={axis: peer}, device_id_type=MESH)
    pl.semaphore_wait(barrier, len(peers))


def gather_row_kernel(clean_ref, corrupt_ref, out_ref, local_sem, send_sem, recv_sem, pair_send, pair_recv):
    me = lax.axis_index("row")
    z, core = me // 2, me % 2
    right = ((z + 1) % ZN) * 2 + core
    left = ((z + ZN - 1) % ZN) * 2 + core
    pair = z * 2 + (1 - core)
    first = pltpu.make_async_copy(clean_ref, out_ref.at[me, 0], local_sem.at[0])
    second = pltpu.make_async_copy(corrupt_ref, out_ref.at[me, 1], local_sem.at[1])
    first.start()
    second.start()
    greet("row", (left, right, pair))
    first.wait()
    second.wait()

    def chain(way, step, block):
        view = out_ref.at[block] if step < 3 else out_ref.at[block, way]
        return remote(view, view, send_sem.at[way, step], recv_sem.at[way, step], "row", (right, left)[way])

    def hand(slot, view):
        return remote(view, view, pair_send.at[slot], pair_recv.at[slot], "row", pair)

    started = []

    def go(copy):
        copy.start()
        started.append(copy)

    go(chain(0, 0, me))
    go(chain(1, 0, me))
    go(hand(0, out_ref.at[me]))
    for step in range(4):
        for way in range(2):
            away = (ZN - step - 1) if way == 0 else (step + 1)
            block = ((z + away) % ZN) * 2 + core
            chain(way, step, block).wait_recv()
            if step < 3:
                go(chain(way, step + 1, block))
            view = out_ref.at[block] if step < 3 else out_ref.at[block, way]
            go(hand(1 + step * 2 + way, view))
    hand(0, out_ref.at[pair]).wait_recv()
    for step in range(4):
        for way in range(2):
            away = (ZN - step - 1) if way == 0 else (step + 1)
            block = ((z + away) % ZN) * 2 + (1 - core)
            view = out_ref.at[block] if step < 3 else out_ref.at[block, way]
            hand(1 + step * 2 + way, view).wait_recv()
    for copy in started:
        copy.wait_send()


def gather_row(clean, corrupt):
    rows, width = clean.shape
    return pl.pallas_call(
        gather_row_kernel,
        out_shape=jax.ShapeDtypeStruct((2 * ZN, 2, rows, width), clean.dtype),
        in_specs=[pl.BlockSpec(memory_space=pl.ANY)] * 2,
        out_specs=pl.BlockSpec(memory_space=pltpu.VMEM),
        scratch_shapes=[
            pltpu.SemaphoreType.DMA((2,)),
            pltpu.SemaphoreType.DMA((2, 4)),
            pltpu.SemaphoreType.DMA((2, 4)),
            pltpu.SemaphoreType.DMA((9,)),
            pltpu.SemaphoreType.DMA((9,)),
        ],
        compiler_params=pltpu.CompilerParams(collective_id=0, has_side_effects=True),
        name="gather_row",
    )(clean, corrupt)


def gather_col_kernel(own_ref, out_ref, local_sem, send_sem, recv_sem):
    me = lax.axis_index("col")
    y, x = me // XN, me % XN
    half = own_ref.shape[1] // 2

    def at(dy, dx):
        return ((y + dy) % XN) * XN + (x + dx) % XN

    local = pltpu.make_async_copy(own_ref, out_ref.at[me], local_sem.at[0])
    local.start()
    greet("col", (at(0, 1), at(0, XN - 1), at(1, 0), at(XN - 1, 0)))
    local.wait()

    started = []

    def neighbour(run, stage, way):
        step = 1 if way == 0 else XN - 1
        along_x = (run + stage) % 2 == 0
        return at(0, step) if along_x else at(step, 0)

    def block_of(run, lane, hop):
        return at(hop, lane) if run == 0 else at(lane, hop)

    def copy_of(run, group, way, far, block):
        stage = 0 if group == 0 else 1
        view = out_ref.at[block, run]
        if far:
            view = out_ref.at[block, run, pl.ds(way * half, half)]
        sems = (run, group, way * 2 + far)
        return remote(view, view, send_sem.at[sems], recv_sem.at[sems], "col", neighbour(run, stage, way))

    def go(*key):
        copy = copy_of(*key)
        copy.start()
        started.append(copy)

    def second(run, lane):
        block = block_of(run, lane, 0)
        for way in range(2):
            go(run, 1 + lane, way, 0, block)

    for run in range(2):
        for way in range(2):
            go(run, 0, way, 0, me)
    for run in range(2):
        second(run, 0)
    for way in range(2):
        lane = XN - 1 if way == 0 else 1
        for run in range(2):
            block = block_of(run, lane, 0)
            copy_of(run, 0, way, 0, block).wait_recv()
            go(run, 0, way, 1, block)
            second(run, lane)

    def relay(run, lane):
        for way in range(2):
            hop = XN - 1 if way == 0 else 1
            block = block_of(run, lane, hop)
            copy_of(run, 1 + lane, way, 0, block).wait_recv()
            go(run, 1 + lane, way, 1, block)

    for run in range(2):
        relay(run, 0)
    for run in range(2):
        block = block_of(run, 2, 0)
        for way in range(2):
            copy_of(run, 0, way, 1, block).wait_recv()
        second(run, 2)
    for lane in (3, 1, 2):
        for run in range(2):
            relay(run, lane)
    for lane in range(XN):
        for run in range(2):
            for way in range(2):
                copy_of(run, 1 + lane, way, 1, block_of(run, lane, 2)).wait_recv()
    for copy in started:
        copy.wait_send()


def gather_col(paired):
    return pl.pallas_call(
        gather_col_kernel,
        out_shape=jax.ShapeDtypeStruct((XN * XN,) + paired.shape, paired.dtype),
        in_specs=[pl.BlockSpec(memory_space=pl.ANY)],
        out_specs=pl.BlockSpec(memory_space=pltpu.VMEM),
        scratch_shapes=[
            pltpu.SemaphoreType.DMA((1,)),
            pltpu.SemaphoreType.DMA((2, 1 + XN, 4)),
            pltpu.SemaphoreType.DMA((2, 1 + XN, 4)),
        ],
        compiler_params=pltpu.CompilerParams(collective_id=1, has_side_effects=True),
        name="gather_col",
    )(paired)


def scatter_row_kernel(part_ref, clean_ref, patched_ref, pair_buf, out_buf, in_buf, pair_send, pair_recv, send_sem, recv_sem):
    me = lax.axis_index("row")
    z, core = me // 2, me % 2
    pair = z * 2 + (1 - core)
    peers = [((z + d) % ZN) * 2 + core for d in range(1, ZN)]
    greet("row", [pair] + peers)
    order = (4, 3, 5, 2, 6, 1, 7, 0)

    def hand(d):
        target = ((z + d) % ZN) * 2 + (1 - core)
        return remote(part_ref.at[target], pair_buf.at[d], pair_send.at[d], pair_recv.at[d], "row", pair)

    def cast(d):
        return remote(out_buf.at[d], in_buf.at[d], send_sem.at[d], recv_sem.at[d], "row", ((z + d) % ZN) * 2 + core)

    for d in order:
        hand(d).start()
    for d in order[:-1]:
        hand(d).wait_recv()
        mine = ((z + d) % ZN) * 2 + core
        out_buf[d] = (part_ref[mine] + pair_buf[d]).astype(out_buf.dtype)
        cast(d).start()
    hand(0).wait_recv()
    total = part_ref[me] + pair_buf[0]
    clean_ref[...] = total[0]
    patched_ref[...] = total[1]
    for d in (1, 7, 2, 6, 3, 5, 4):
        cast(d).wait_recv()
        clean_ref[...] += in_buf[d, 0].astype(jnp.float32)
        patched_ref[...] += in_buf[d, 1].astype(jnp.float32)
    for d in range(ZN):
        hand(d).wait_send()
    for d in range(1, ZN):
        cast(d).wait_send()


def scatter_row(part):
    block = part.shape[1:]
    out = jax.ShapeDtypeStruct(block[1:], jnp.float32)
    return pl.pallas_call(
        scatter_row_kernel,
        out_shape=(out, out),
        in_specs=[pl.BlockSpec(memory_space=pltpu.VMEM)],
        out_specs=(pl.BlockSpec(memory_space=pltpu.VMEM), pl.BlockSpec(memory_space=pltpu.VMEM)),
        scratch_shapes=[
            pltpu.VMEM((ZN,) + block, jnp.float32),
            pltpu.VMEM((ZN,) + block, jnp.bfloat16),
            pltpu.VMEM((ZN,) + block, jnp.bfloat16),
            pltpu.SemaphoreType.DMA((ZN,)),
            pltpu.SemaphoreType.DMA((ZN,)),
            pltpu.SemaphoreType.DMA((ZN,)),
            pltpu.SemaphoreType.DMA((ZN,)),
        ],
        compiler_params=pltpu.CompilerParams(collective_id=2, has_side_effects=True),
        name="scatter_row",
    )(part)


def scatter_col_kernel(gate_ref, up_ref, gate_out, up_out, far, free, dep, mid, far2, free2, dep2, send1, recv1, send2, recv2):
    me = lax.axis_index("col")
    y, x = me // XN, me % XN
    parts, outs = (gate_ref, up_ref), (gate_out, up_out)
    half = gate_ref.shape[1] // 2
    rows = (pl.ds(0, half), pl.ds(half, half))
    lanes = (1, XN - 1)

    def at(dy, dx):
        return ((y + dy) % XN) * XN + (x + dx) % XN

    def block(run, lane, hop):
        return at(hop, lane) if run == 0 else at(lane, hop)

    started = []

    def go(copy):
        copy.start()
        started.append(copy)

    def first(kind, run, way, j):
        if kind == 0:
            src, dst = parts[run].at[block(run, 2, j), rows[way]], far.at[run, way, j]
        elif kind == 1:
            src, dst = far.at[run, way, j], dep.at[run, way, j]
        else:
            src, dst = parts[run].at[block(run, lanes[way], j), rows[1 - way]], free.at[run, way, j]
        sems = (kind, run, way, j)
        return remote(src, dst, send1.at[sems], recv1.at[sems], "col", block(run, lanes[way], 0))

    def second(kind, run, way):
        if kind == 0:
            src, dst = mid.at[run, 2, rows[way]], far2.at[run, way]
        elif kind == 1:
            src, dst = far2.at[run, way], dep2.at[run, way]
        else:
            src, dst = mid.at[run, lanes[way], rows[1 - way]], free2.at[run, way]
        sems = (kind, run, way)
        return remote(src, dst, send2.at[sems], recv2.at[sems], "col", block(run, 0, lanes[way]))

    both = [(run, way) for way in range(2) for run in range(2)]

    def passes(j):
        for run, way in both:
            first(0, run, way, j).wait_recv()
            far[run, way, j] += parts[run][block(run, lanes[way], j), rows[way]]
            go(first(1, run, way, j))
        for run, way in both:
            go(first(2, run, way, j))

    def totals(j):
        for run, way in both:
            first(1, run, way, j).wait_recv()
            first(2, run, way, j).wait_recv()
        for run in range(2):
            mine = block(run, 0, j)
            for way in range(2):
                mid[run, j, rows[way]] = parts[run][mine, rows[way]] + dep[run, way, j] + free[run, 1 - way, j]

    greet("col", (at(0, 1), at(0, XN - 1), at(1, 0), at(XN - 1, 0)))
    for j in (2, 1):
        for run, way in both:
            go(first(0, run, way, j))
    passes(2)
    for run, way in both:
        go(first(0, run, way, 3))
    passes(1)
    for run, way in both:
        go(first(0, run, way, 0))
    passes(3)
    totals(2)
    for run, way in both:
        go(second(0, run, way))
    passes(0)
    totals(1)
    for run in range(2):
        go(second(2, run, 0))
    totals(3)
    for run in range(2):
        go(second(2, run, 1))
    for run, way in both:
        second(0, run, way).wait_recv()
        far2[run, way] += mid[run, lanes[way], rows[way]]
        go(second(1, run, way))
    totals(0)
    for run, way in both:
        second(1, run, way).wait_recv()
        second(2, run, way).wait_recv()
    for run, way in both:
        outs[run][rows[way]] = mid[run, 0, rows[way]] + dep2[run, way] + free2[run, 1 - way]
    for copy in started:
        copy.wait_send()


def scatter_col(gate_part, up_part):
    count, rows, width = gate_part.shape
    out = jax.ShapeDtypeStruct((rows, width), jnp.float32)
    wide = pltpu.VMEM((2, 2, XN, rows // 2, width), jnp.float32)
    slim = pltpu.VMEM((2, 2, rows // 2, width), jnp.float32)
    vmem = pl.BlockSpec(memory_space=pltpu.VMEM)
    return pl.pallas_call(
        scatter_col_kernel,
        out_shape=(out, out),
        in_specs=[vmem, vmem],
        out_specs=(vmem, vmem),
        scratch_shapes=[
            wide, wide, wide,
            pltpu.VMEM((2, XN, rows, width), jnp.float32),
            slim, slim, slim,
            pltpu.SemaphoreType.DMA((3, 2, 2, XN)),
            pltpu.SemaphoreType.DMA((3, 2, 2, XN)),
            pltpu.SemaphoreType.DMA((3, 2, 2)),
            pltpu.SemaphoreType.DMA((3, 2, 2)),
        ],
        compiler_params=pltpu.CompilerParams(collective_id=3, has_side_effects=True, vmem_limit_bytes=48 << 20),
        name="scatter_col",
    )(gate_part, up_part)


def on_device(clean_in, corrupt_in, patch_mask, gate_weight, up_weight, down_weight):
    rows, width = clean_in.shape
    piece = gather_row(clean_in, corrupt_in).reshape(-1, width)
    gate_part = jnp.dot(piece, gate_weight, preferred_element_type=jnp.float32)
    up_part = jnp.dot(piece, up_weight, preferred_element_type=jnp.float32)
    split = (XN * XN, 2 * rows, -1)
    gate, up = scatter_col(gate_part.reshape(split), up_part.reshape(split))
    row_mask = lax.dynamic_slice_in_dim(patch_mask, lax.axis_index("col") * rows, rows, 0)
    hidden = (jax.nn.silu(gate) * up).astype(jnp.bfloat16).reshape(2, rows, -1)
    patched = jnp.where(row_mask[:, None] == 1, hidden[0], hidden[1])
    gathered = gather_col(jnp.stack((hidden[0], patched)))
    part = jnp.dot(gathered.reshape(-1, gathered.shape[-1]), down_weight, preferred_element_type=jnp.float32)
    return scatter_row(part.reshape(2 * ZN, 2, rows, -1))


def solution(mesh):
    placed = (
        P("row", "col"),
        P("row", "col"),
        P(),
        P("col", "row"),
        P("col", "row"),
        P("row", "col"),
    )
    return jax.shard_map(
        on_device,
        mesh=mesh,
        in_specs=placed,
        out_specs=(P("row", "col"), P("row", "col")),
        check_vma=False,
    )
```
